32 devices in a mesh: fsdp: 2 (over x), ctx: 4 (over z), tp: 4 (over y, core).
Axes of the slice: x: 2, y: 2, z: 4, core: 2. Of those that a mesh axis runs over, the one named last changes fastest.
Arguments:
- layer_input: bfloat16 [4, 1024, 2048], P('fsdp', 'ctx'), may hold values from -6 to 6
- cotangent: bfloat16 [4, 1024, 2048], P('fsdp', 'ctx'), may hold values from -6 to 6
- lengths: int32 [4], P('fsdp'), may hold values from 256 to 1024, as said below
- w_query: bfloat16 [2048, 2048], P('fsdp', 'tp'), may hold values from -0.125 to 0.125
- w_key: bfloat16 [2048, 2048], P('fsdp', 'tp'), may hold values from -0.125 to 0.125
- w_value: bfloat16 [2048, 2048], P('fsdp', 'tp'), may hold values from -0.125 to 0.125
- w_attn_out: bfloat16 [2048, 2048], P('tp', 'fsdp'), may hold values from -0.5 to 0.5
- w_gate: bfloat16 [2048, 8192], P('fsdp', 'tp'), may hold values from -0.125 to 0.125
- w_up: bfloat16 [2048, 8192], P('fsdp', 'tp'), may hold values from -0.125 to 0.125
- w_down: bfloat16 [8192, 2048], P('tp', 'fsdp'), may hold values from -0.0625 to 0.0625
Outputs:
- out_block: bfloat16 [4, 1024, 2048], P('fsdp', 'ctx')
- grad_input: float32 [4, 1024, 2048], P('fsdp', 'ctx')
- grad_query: float32 [2048, 2048], P('fsdp', 'tp')
- grad_key: float32 [2048, 2048], P('fsdp', 'tp')
- grad_value: float32 [2048, 2048], P('fsdp', 'tp')
- grad_attn_out: float32 [2048, 2048], P('tp', 'fsdp')
- grad_gate: float32 [2048, 8192], P('fsdp', 'tp')
- grad_up: float32 [2048, 8192], P('fsdp', 'tp')
- grad_down: float32 [8192, 2048], P('tp', 'fsdp')
The draws below stay inside these ranges and needn't reach their ends.
Inputs may be any that keep to these rules, and one draw needn't show every extreme that they name: Each sequence's used slots are its first lengths[s]; some sequence is full in every draw.
All inputs are finite; a program needn't handle non-finite values.
Results may differ from the reference program's by a relative error of at most 0.015.
Values may be sent and summed in bfloat16 or wider, within the bound.
No kernel may reach another device: no remote copies, remote signals or barrier semaphores. Data moves between devices by JAX's collectives and lax.ppermute only.
A program may use at most 256 MiB of HBM per device.

```python
from functools import partial
import jax
import jax.numpy as jnp
from jax import lax

D = 2048
HEADS = 16
HD = 128
FF = 8192
SEQ = 1024
MIN_LEN = 256
SEQS = 4


def draw_lengths(key, part):
    first = jax.random.fold_in(key, 11)
    second = jax.random.fold_in(key, 12)
    base = jax.random.randint(first, (SEQS,), MIN_LEN, SEQ + 1)
    chosen = jax.random.randint(second, (), 0, SEQS)
    return jnp.where(jnp.arange(SEQS) == chosen, SEQ, base).astype(jnp.int32)


def level_of(stream_key, dims, split, least, largest):
    gain = 1.0
    for axis_at, parts in split:
        heights = jax.random.uniform(jax.random.fold_in(jax.random.fold_in(stream_key, 6), axis_at), (parts,), jnp.float32, least / len(split), largest / len(split))
        gain = gain * jnp.repeat(jnp.exp(heights), dims[axis_at] // parts).reshape((-1,) + (1,) * (len(dims) - 1 - axis_at))
    return gain


def gaussian(rng, extent, width, bound, split=(), held_as=jnp.bfloat16):
    level = level_of(rng, extent, split, -0.22, 0.18) if split else 1.0
    array = jax.random.normal(rng, extent, jnp.float32) * width * level
    return jnp.minimum(jnp.maximum(array, -bound), bound).astype(held_as)


def setup_inputs(seed: int = 0) -> dict:
    key_list = jax.random.split(jax.random.key(seed), 11)
    return {
        "layer_input": gaussian(key_list[0], (SEQS, SEQ, D), 1.0, 6.0, ((0, 2), (1, 4))),
        "cotangent": gaussian(key_list[1], (SEQS, SEQ, D), 1.0, 6.0, ((0, 2), (1, 4))),
        "lengths": draw_lengths(jax.random.fold_in(key_list[10], 71), 0),
        "w_query": gaussian(key_list[3], (D, D), D ** -0.5, 0.125, ((0, 2), (1, 4))),
        "w_key": gaussian(key_list[4], (D, D), D ** -0.5, 0.125, ((0, 2), (1, 4))),
        "w_value": gaussian(key_list[5], (D, D), D ** -0.5, 0.125, ((0, 2), (1, 4))),
        "w_attn_out": gaussian(key_list[6], (D, D), (D // 16) ** -0.5, 0.5, ((0, 4), (1, 2))),
        "w_gate": gaussian(key_list[7], (D, FF), D ** -0.5, 0.125, ((0, 2), (1, 4))),
        "w_up": gaussian(key_list[8], (D, FF), D ** -0.5, 0.125, ((0, 2), (1, 4))),
        "w_down": gaussian(key_list[9], (FF, D), FF ** -0.5, 0.0625, ((0, 4), (1, 2))),
    }


@jax.custom_vjp
def low(v):
    return lax.optimization_barrier(v.astype(jnp.bfloat16)).astype(jnp.float32)

@jax.custom_vjp
def low_back(v):
    return v

def low_keep(v):
    return (low(v), None)

def low_pass(kept, grad):
    return (grad,)

def back_keep(v):
    return (v, None)

def back_low(kept, grad):
    return (low(grad),)
low.defvjp(low_keep, low_pass)
low_back.defvjp(back_keep, back_low)

def layer_norm(v):
    centered = v - lax.optimization_barrier(jnp.mean(v, axis=-1, keepdims=True))
    return centered * lax.rsqrt(lax.optimization_barrier(jnp.mean(centered * centered, axis=-1, keepdims=True)) + 1e-05)

def tables():
    freqs = 10000.0 ** (-(jnp.arange(HD // 2, dtype=jnp.float32) * 2.0) / HD)
    angles = jnp.arange(SEQ, dtype=jnp.float32)[:, None] * freqs[None, :]
    angles = jnp.concatenate([angles, angles], axis=-1)
    return (jnp.cos(angles)[None, :, None, :], jnp.sin(angles)[None, :, None, :])

def rotary(v, cosine, sine):
    turned = jnp.concatenate([-v[..., HD // 2:], v[..., :HD // 2]], axis=-1)
    return v * cosine + turned * sine

def attend(args):
    queries, keys, values, length = args
    highest = lax.Precision.HIGHEST
    scores = jnp.einsum('qhd,khd->hqk', queries, keys, precision=highest) / jnp.sqrt(jnp.float32(HD))
    scores = low_back(scores)
    places = jnp.arange(SEQ)
    visible = (places[None, :] <= places[:, None]) & (places[None, :] < length)
    masked = jnp.where(visible[None], scores, -1e+30)
    top = lax.optimization_barrier(jnp.max(masked, axis=-1, keepdims=True))
    expo = jnp.where(visible[None], jnp.exp(masked - top), 0.0)
    probs = low(expo / lax.optimization_barrier(jnp.sum(expo, axis=-1, keepdims=True)))
    return jnp.einsum('hqk,khd->qhd', probs, values, precision=highest)

def forward(lengths, xf, w_query, w_key, w_value, w_attn_out, w_gate, w_up, w_down):
    highest = lax.Precision.HIGHEST
    nseq = xf.shape[0]

    def matmul(a, b):
        return jnp.dot(a, b, precision=highest)
    rows_x = xf.reshape(-1, D)
    u1 = low(layer_norm(rows_x))
    cosine, sine = tables()
    qraw = low_back(matmul(u1, w_query)).reshape(nseq, SEQ, HEADS, HD)
    kraw = low_back(matmul(u1, w_key)).reshape(nseq, SEQ, HEADS, HD)
    values = low(low_back(matmul(u1, w_value))).reshape(nseq, SEQ, HEADS, HD)
    queries = low(rotary(qraw, cosine, sine))
    keys = low(rotary(kraw, cosine, sine))
    attended = lax.map(jax.checkpoint(attend), (queries, keys, values, lengths))
    context = low(low_back(attended.reshape(-1, D)))
    h1 = rows_x + low_back(matmul(context, w_attn_out))
    u2 = low(layer_norm(h1))
    gate = low_back(matmul(u2, w_gate))
    upper = low_back(matmul(u2, w_up))
    hidden = low(jax.nn.silu(gate) * upper)
    h2 = h1 + matmul(hidden, w_down)
    keep = (jnp.arange(SEQ)[None, :] < lengths[:, None]).astype(jnp.float32).reshape(-1, 1)
    return (h2 * keep).reshape(nseq, SEQ, D)

def reference(layer_input, cotangent, lengths, w_query, w_key, w_value, w_attn_out, w_gate, w_up, w_down):
    floats = [v.astype(jnp.float32) for v in (layer_input, w_query, w_key, w_value, w_attn_out, w_gate, w_up, w_down)]
    result, pullback = jax.vjp(partial(forward, lengths), *floats)
    grads = pullback(cotangent.astype(jnp.float32))
    return (result.astype(jnp.bfloat16), grads[0], grads[1], grads[2], grads[3], grads[4], grads[5], grads[6], grads[7])
```

```python
import jax
import jax.numpy as jnp
from jax import lax
from jax.sharding import PartitionSpec as P

HD = 128
BF = jnp.bfloat16
F32 = jnp.float32


def layer_norm(v):
    centered = v - jnp.mean(v, axis=-1, keepdims=True)
    rstd = lax.rsqrt(jnp.mean(centered * centered, axis=-1, keepdims=True) + 1e-05)
    return (centered * rstd, rstd)


def norm_back(grad, normed, rstd):
    return rstd * (
        grad
        - jnp.mean(grad, axis=-1, keepdims=True)
        - normed * jnp.mean(grad * normed, axis=-1, keepdims=True)
    )


def rotary(v, cosine, sine, half):
    turned = jnp.concatenate([-v[..., half:], v[..., :half]], axis=-1)
    return v * cosine + turned * sine


def rotary_back(grad, cosine, sine, half):
    scaled = grad * sine
    return grad * cosine + jnp.concatenate([scaled[..., half:], -scaled[..., :half]], axis=-1)


def dot(left, right):
    return jnp.dot(left, right, preferred_element_type=F32)


def tdot(left, right):
    return lax.dot_general(left, right, (((0,), (0,)), ((), ())), preferred_element_type=F32)


def ndot(left, right):
    return lax.dot_general(left, right, (((1,), (1,)), ((), ())), preferred_element_type=F32)


def swap_fsdp(v):
    return lax.ppermute(v, "fsdp", [(0, 1), (1, 0)])


def tp_swap(v, bit):
    n = lax.axis_size("tp")
    return lax.ppermute(v, "tp", [(i, i ^ bit) for i in range(n)])


def tp_total(term):
    n = lax.axis_size("tp")
    odd = (lax.axis_index("tp") & 1) == 1
    mid = term.shape[0] // 2
    low, high = term[:mid], term[mid:]
    mine = jnp.where(odd, high, low)
    total = mine + tp_swap(jnp.where(odd, low, high).astype(BF), 1).astype(F32)
    bit = 2
    while bit < n:
        sent = total.astype(BF)
        total = sent.astype(F32) + tp_swap(sent, bit).astype(F32)
        bit *= 2
    kept = total.astype(BF)
    other = tp_swap(kept, 1)
    return jnp.where(
        odd, jnp.concatenate([other, kept], axis=0), jnp.concatenate([kept, other], axis=0)
    ).astype(F32)


def ctx_total(v):
    place = lax.axis_index("ctx")
    first = (v.astype(F32) + lax.ppermute(v, "ctx", [(0, 1), (3, 2)]).astype(F32)).astype(BF)
    both = first.astype(F32) + lax.ppermute(first, "ctx", [(1, 2), (2, 1)]).astype(F32)
    both = both.astype(BF)
    back = lax.ppermute(both, "ctx", [(1, 0), (2, 3)])
    return jnp.where((place == 0) | (place == 3), back, both).astype(F32)


def reduce_grad(own, other):
    got = swap_fsdp(other.astype(BF))
    return ctx_total((own + got.astype(F32)).astype(BF))


def turn(v, flip):
    half = v.shape[-1] // 2
    return jnp.where(flip, jnp.concatenate([v[..., half:], v[..., :half]], axis=-1), v)


def per_device(
    layer_input, cotangent, lengths, w_query, w_key, w_value, w_attn_out, w_gate, w_up, w_down
):
    nseq, local, width = layer_input.shape
    dh = width // 2
    rows = nseq * local
    whole = local * lax.axis_size("ctx")
    flip = lax.axis_index("fsdp") == 1
    places = lax.axis_index("ctx") * local + jnp.arange(local, dtype=jnp.int32)
    every = jnp.arange(whole, dtype=jnp.int32)
    half = HD // 2
    freqs = 10000.0 ** (-(jnp.arange(half, dtype=F32) * 2.0) / HD)
    angles = places.astype(F32)[:, None] * freqs[None, :]
    angles = jnp.concatenate([angles, angles], axis=-1)
    cosine = jnp.cos(angles)[None, :, None, :]
    sine = jnp.sin(angles)[None, :, None, :]
    factor = 1.0 / jnp.sqrt(F32(HD))
    own = (w_query, w_key, w_value, w_attn_out, w_gate, w_up, w_down)
    oth = [None] * 7
    for i in (1, 2, 0, 3, 4, 5, 6):
        oth[i] = swap_fsdp(own[i])
    heads = w_query.shape[1] // HD
    xf = turn(layer_input, flip).astype(F32).reshape(rows, width)
    n1, rstd1 = layer_norm(xf)
    u1 = n1.astype(BF)

    def into(u, i):
        return dot(u[:, :dh], own[i]) + dot(u[:, dh:], oth[i])

    def out_of(u, i):
        return jnp.concatenate([dot(u, own[i]), dot(u, oth[i])], axis=1)

    def into_back(g, i):
        return jnp.concatenate([ndot(g, own[i]), ndot(g, oth[i])], axis=1)

    def out_back(g, i):
        return ndot(g[:, :dh], own[i]) + ndot(g[:, dh:], oth[i])

    kraw = into(u1, 1).reshape(nseq, local, heads, HD)
    vlocal = into(u1, 2).astype(BF).reshape(nseq, local, heads, HD)
    qraw = into(u1, 0).reshape(nseq, local, heads, HD)
    queries = rotary(qraw, cosine, sine, half).astype(BF)
    klocal = rotary(kraw, cosine, sine, half).astype(BF)
    kv = lax.all_gather(jnp.concatenate([klocal, vlocal], axis=2), "ctx", axis=1, tiled=True)
    keys, values = kv[:, :, :heads], kv[:, :, heads:]
    scores = (
        jnp.einsum("sqhd,skhd->shqk", queries, keys, preferred_element_type=F32) * factor
    )
    visible = (every[None, None, :] <= places[None, :, None]) & (
        every[None, None, :] < lengths[:, None, None]
    )
    visible = visible[:, None, :, :]
    masked = jnp.where(visible, scores, -1e30)
    top = jnp.max(masked, axis=-1, keepdims=True)
    expo = jnp.where(visible, jnp.exp(masked - top), 0.0)
    probs = expo / jnp.sum(expo, axis=-1, keepdims=True)
    probs_low = probs.astype(BF)
    attended = jnp.einsum("shqk,skhd->sqhd", probs_low, values, preferred_element_type=F32)
    context = attended.astype(BF).reshape(rows, heads * HD)
    keep = (places[None, :] < lengths[:, None]).astype(F32).reshape(rows, 1)
    dy = turn(cotangent, flip).astype(F32).reshape(rows, width) * keep
    dy_low = dy.astype(BF)
    h1 = xf + tp_total(out_of(context, 3))
    n2, rstd2 = layer_norm(h1)
    u2 = n2.astype(BF)
    gate = into(u2, 4)
    upper = into(u2, 5)
    sigma = jax.nn.sigmoid(gate)
    hidden = (gate * sigma * upper).astype(BF)

    ff = hidden.shape[1]
    cut = ff // 2

    def grad_into(u, g):
        return reduce_grad(tdot(u[:, :dh], g), tdot(u[:, dh:], g))

    def grad_out(u, g):
        return reduce_grad(tdot(u, g[:, :dh]), tdot(u, g[:, dh:]))

    g_down = jnp.concatenate(
        [grad_out(hidden[:, :cut], dy_low), grad_out(hidden[:, cut:], dy_low)], axis=0
    )
    dhidden = out_back(dy_low, 6)
    dgate = (dhidden * upper * sigma * (1.0 + gate * (1.0 - sigma))).astype(BF)
    dupper = (dhidden * gate * sigma).astype(BF)
    du2_term = jnp.concatenate(
        [
            ndot(dgate, own[4]) + ndot(dupper, own[5]),
            ndot(dgate, oth[4]) + ndot(dupper, oth[5]),
        ],
        axis=1,
    )
    dh1 = dy + norm_back(tp_total(du2_term), n2, rstd2)
    g_gate = jnp.concatenate(
        [grad_into(u2, dgate[:, :cut]), grad_into(u2, dgate[:, cut:])], axis=1
    )
    g_up = jnp.concatenate(
        [grad_into(u2, dupper[:, :cut]), grad_into(u2, dupper[:, cut:])], axis=1
    )
    h2 = h1 + tp_total(out_of(hidden, 6))
    out_block = turn((h2 * keep).astype(BF), flip)
    da_low = dh1.astype(BF)
    g_attn = grad_out(context, da_low)
    dcontext = out_back(da_low, 3).astype(BF).reshape(nseq, local, heads, HD)
    dprobs = jnp.einsum("sqhd,skhd->shqk", dcontext, values, preferred_element_type=F32)
    delta = jnp.sum(probs * dprobs, axis=-1, keepdims=True)
    dscores = (probs * (dprobs - delta)).astype(BF)
    dq_rot = (
        jnp.einsum("shqk,skhd->sqhd", dscores, keys, preferred_element_type=F32) * factor
    )
    dk_all = (
        jnp.einsum("shqk,sqhd->skhd", dscores, queries, preferred_element_type=F32) * factor
    )
    dv_all = jnp.einsum("shqk,sqhd->skhd", probs_low, dcontext, preferred_element_type=F32)
    dkv = lax.psum_scatter(
        jnp.concatenate([dk_all.astype(BF), dv_all.astype(BF)], axis=2),
        "ctx",
        scatter_dimension=1,
        tiled=True,
    )
    dk_rot, dv_low = dkv[:, :, :heads].astype(F32), dkv[:, :, heads:].reshape(rows, heads * HD)
    dq_low = rotary_back(dq_rot, cosine, sine, half).astype(BF).reshape(rows, heads * HD)
    dk_low = rotary_back(dk_rot, cosine, sine, half).astype(BF).reshape(rows, heads * HD)
    g_query = grad_into(u1, dq_low)
    g_key = grad_into(u1, dk_low)
    g_value = grad_into(u1, dv_low)
    du1_term = jnp.concatenate(
        [
            ndot(dq_low, w[0]) + ndot(dk_low, w[1]) + ndot(dv_low, w[2])
            for w in (own, oth)
        ],
        axis=1,
    )
    grad_input = turn(dh1 + norm_back(tp_total(du1_term), n1, rstd1), flip)
    return (
        out_block.reshape(nseq, local, width),
        grad_input.reshape(nseq, local, width),
        g_query,
        g_key,
        g_value,
        g_attn,
        g_gate,
        g_up,
        g_down,
    )


def solution(mesh):
    return jax.shard_map(
        per_device,
        mesh=mesh,
        in_specs=(
            P("fsdp", "ctx", None),
            P("fsdp", "ctx", None),
            P("fsdp"),
            P("fsdp", "tp"),
            P("fsdp", "tp"),
            P("fsdp", "tp"),
            P("tp", "fsdp"),
            P("fsdp", "tp"),
            P("fsdp", "tp"),
            P("tp", "fsdp"),
        ),
        out_specs=(
            P("fsdp", "ctx", None),
            P("fsdp", "ctx", None),
            P("fsdp", "tp"),
            P("fsdp", "tp"),
            P("fsdp", "tp"),
            P("tp", "fsdp"),
            P("fsdp", "tp"),
            P("fsdp", "tp"),
            P("tp", "fsdp"),
        ),
        check_vma=False,
    )
```

```python
import jax
import jax.numpy as jnp
from jax import lax
from jax.experimental import pallas as pl
from jax.experimental.pallas import tpu as pltpu
from jax.sharding import PartitionSpec as P

HD = 128
BF = jnp.bfloat16
F32 = jnp.float32


def layer_norm(v):
    centered = v - jnp.mean(v, axis=-1, keepdims=True)
    rstd = lax.rsqrt(jnp.mean(centered * centered, axis=-1, keepdims=True) + 1e-05)
    return (centered * rstd, rstd)


def norm_back(grad, normed, rstd):
    return rstd * (
        grad
        - jnp.mean(grad, axis=-1, keepdims=True)
        - normed * jnp.mean(grad * normed, axis=-1, keepdims=True)
    )


def dot(left, right):
    return jnp.dot(left, right, preferred_element_type=F32)


def tdot(left, right):
    return lax.dot_general(left, right, (((0,), (0,)), ((), ())), preferred_element_type=F32)


def ndot(left, right):
    return lax.dot_general(left, right, (((1,), (1,)), ((), ())), preferred_element_type=F32)


def mm(left, right, dims):
    return lax.dot_general(left, right, (dims, ((), ())), preferred_element_type=F32)


def block_probs(q, k, length, first):
    span = (q.shape[0], k.shape[0])
    scores = mm(q, k, ((1,), (1,))) * (1.0 / HD**0.5)
    query = first + lax.broadcasted_iota(jnp.int32, span, 0)
    key = lax.broadcasted_iota(jnp.int32, span, 1)
    visible = (key <= query) & (key < length)
    masked = jnp.where(visible, scores, -1e30)
    top = jnp.max(masked, axis=-1, keepdims=True)
    expo = jnp.where(visible, jnp.exp(masked - top), 0.0)
    return expo / jnp.sum(expo, axis=-1, keepdims=True)


def forward_body(block, lens, qraw, kraw, v, cosine, sine, qr, kr, ctx):
    length = lens[pl.program_id(0)]
    for raw, out in ((qraw, qr), (kraw, kr)):
        x = raw[...]
        out[...] = (x * cosine[...] + pltpu.roll(x, HD // 2, 1) * sine[...]).astype(BF)
    for first in range(0, qr.shape[0], block):
        last = first + block
        probs = block_probs(qr[first:last, :], kr[:last, :], length, first).astype(BF)
        ctx[first:last, :] = mm(probs, v[:last, :], ((1,), (0,))).astype(BF)


def backward_body(block, lens, qr, kr, v, dctx, cosine, sine, dq, dk, dv, dk_sum, dv_sum):
    length = lens[pl.program_id(0)]
    factor = 1.0 / HD**0.5
    dk_sum[...] = jnp.zeros_like(dk_sum)
    dv_sum[...] = jnp.zeros_like(dv_sum)

    def unturn(x, c, s):
        return (x * c - pltpu.roll(x, HD // 2, 1) * s).astype(BF)

    for first in range(0, qr.shape[0], block):
        last = first + block
        q = qr[first:last, :]
        dc = dctx[first:last, :]
        k = kr[:last, :]
        probs = block_probs(q, k, length, first)
        dprobs = mm(dc, v[:last, :], ((1,), (1,)))
        delta = jnp.sum(probs * dprobs, axis=-1, keepdims=True)
        dscores = (probs * (dprobs - delta)).astype(BF)
        dq[first:last, :] = unturn(
            mm(dscores, k, ((1,), (0,))) * factor, cosine[first:last, :], sine[first:last, :]
        )
        dk_sum[:last, :] += mm(dscores, q, ((0,), (0,)))
        dv_sum[:last, :] += mm(probs.astype(BF), dc, ((0,), (0,)))
    dk[...] = unturn(dk_sum[...] * factor, cosine[...], sine[...])
    dv[...] = dv_sum[...].astype(BF)


def attention_call(body, lengths, arrays, tables, outs, scratch, name):
    rows, width = arrays[0].shape
    nseq = lengths.shape[0]
    whole = rows // nseq
    tile = pl.BlockSpec((whole, HD), lambda s, h, lens: (s, h))
    table = pl.BlockSpec((whole, HD), lambda s, h, lens: (0, 0))
    block = whole // 4
    return pl.pallas_call(
        lambda *refs: body(block, *refs),
        grid_spec=pltpu.PrefetchScalarGridSpec(
            num_scalar_prefetch=1,
            grid=(nseq, width // HD),
            in_specs=[tile] * len(arrays) + [table] * len(tables),
            out_specs=[tile] * outs,
            scratch_shapes=[pltpu.VMEM((whole, HD), F32)] * scratch,
        ),
        out_shape=[jax.ShapeDtypeStruct((rows, width), BF)] * outs,
        name=name,
    )(lengths, *arrays, *tables)


def swap_fsdp(v):
    return lax.ppermute(v, "fsdp", [(0, 1), (1, 0)])


def tp_swap(v, bit):
    n = lax.axis_size("tp")
    return lax.ppermute(v, "tp", [(i, i ^ bit) for i in range(n)])


def tp_half(make, *parts):
    n = lax.axis_size("tp")
    odd = lax.axis_index("tp") & 1
    mid = parts[0].shape[0] // 2

    def pick(which):
        return make(*(lax.dynamic_slice_in_dim(p, which * mid, mid, 0) for p in parts))

    got = tp_swap(pick(1 - odd).astype(BF), 1)
    total = pick(odd) + got.astype(F32)
    bit = 2
    while bit < n:
        sent = total.astype(BF)
        total = sent.astype(F32) + tp_swap(sent, bit).astype(F32)
        bit *= 2
    return total.astype(BF)


def tp_join(kept):
    odd = lax.axis_index("tp") & 1
    other = tp_swap(kept, 1)
    return jnp.where(
        odd == 1, jnp.concatenate([other, kept], axis=0), jnp.concatenate([kept, other], axis=0)
    ).astype(F32)


def tp_total(make, *parts):
    return tp_join(tp_half(make, *parts))


def line_gather(piece):
    me = lax.axis_index("ctx")
    if lax.axis_size("ctx") != 4:
        return lax.all_gather(piece, "ctx", axis=0, tiled=False)
    up1 = lax.ppermute(piece, "ctx", [(0, 1), (1, 2), (2, 3)])
    down1 = lax.ppermute(piece, "ctx", [(1, 0), (2, 1), (3, 2)])
    up2 = lax.ppermute(piece, "ctx", [(0, 2), (1, 3)])
    down2 = lax.ppermute(piece, "ctx", [(2, 0), (3, 1)])
    far = lax.ppermute(jnp.where(me == 2, up2, down2), "ctx", [(2, 3), (1, 0)])
    box = jnp.zeros((4,) + piece.shape, piece.dtype)
    for s, got in (
        (0, piece),
        (1, jnp.where(me >= 1, up1, far)),
        (2, jnp.where(me >= 2, up2, down2)),
        (3, jnp.where(me == 3, far, down1)),
    ):
        box = lax.dynamic_update_slice_in_dim(box, got[None], (me - s) % 4, 0)
    return box


def spread_weight(piece):
    got = line_gather(swap_fsdp(piece))
    return got.reshape((-1,) + got.shape[2:])


def quarter(w):
    part = w.shape[0] // lax.axis_size("ctx")
    return lax.dynamic_slice_in_dim(w, lax.axis_index("ctx") * part, part, 0)


def spread_rows(piece):
    t = lax.axis_index("tp")
    line = line_gather(piece)
    other = tp_swap(line, 2)
    pair = jnp.where(
        (t & 2) == 2, jnp.stack([other, line], axis=1), jnp.stack([line, other], axis=1)
    )
    other = tp_swap(pair, 1)
    full = jnp.where(
        (t & 1) == 1, jnp.stack([other, pair], axis=0), jnp.stack([pair, other], axis=0)
    )
    return full.reshape(-1, piece.shape[-1])


def run_stream(chunks):
    place = lax.axis_index("ctx")
    edge = (place == 0) | (place == 3)
    n = len(chunks)
    stage1, stage2, stage3, done = {}, {}, {}, []
    for tick in range(n + 3):
        send = {}
        if tick < n:
            send["x"] = chunks[tick][1]
        if 0 <= tick - 1 < n:
            send["a"] = stage1[tick - 1]
        if 0 <= tick - 2 < n:
            send["b"] = stage2[tick - 2]
        if 0 <= tick - 3 < n:
            send["c"] = stage3[tick - 3]
        send = lax.optimization_barrier(send)
        if "c" in send:
            back = lax.ppermute(send["c"], "ctx", [(1, 0), (2, 3)])
            done.append(jnp.where(edge, back, send["c"]))
        if "b" in send:
            got = lax.ppermute(send["b"], "ctx", [(1, 2), (2, 1)])
            stage3[tick - 2] = (send["b"].astype(F32) + got.astype(F32)).astype(BF)
        if "a" in send:
            got = lax.ppermute(send["a"], "ctx", [(0, 1), (3, 2)])
            stage2[tick - 1] = (send["a"].astype(F32) + got.astype(F32)).astype(BF)
        if "x" in send:
            got = swap_fsdp(send["x"])
            stage1[tick] = (chunks[tick][0] + got.astype(F32)).astype(BF)
    return done


def turn(v, flip):
    half = v.shape[-1] // 2
    return jnp.where(flip, jnp.concatenate([v[..., half:], v[..., :half]], axis=-1), v)


def per_device(
    layer_input, cotangent, lengths, w_query, w_key, w_value, w_attn_out, w_gate, w_up, w_down
):
    nseq, local, width = layer_input.shape
    dh = width // 2
    rows = nseq * local
    whole = local * lax.axis_size("ctx")
    flip = lax.axis_index("fsdp") == 1
    me = lax.axis_index("ctx")
    places = me * local + jnp.arange(local, dtype=jnp.int32)
    half = HD // 2
    freqs = 10000.0 ** (-(jnp.arange(half, dtype=F32) * 2.0) / HD)
    angles = jnp.arange(whole, dtype=F32)[:, None] * freqs[None, :]
    cosine = jnp.cos(angles)
    sine = jnp.sin(angles)
    tables = (
        jnp.concatenate([cosine, cosine], axis=-1),
        jnp.concatenate([-sine, sine], axis=-1),
    )
    own = (w_query, w_key, w_value, w_attn_out, w_gate, w_up, w_down)
    x = layer_input.reshape(rows, width)
    t = lax.axis_index("tp")
    fourth = rows // 4

    def my_fourth(v):
        return lax.dynamic_slice_in_dim(v, ((t & 1) * 2 + ((t >> 1) & 1)) * fourth, fourth, 0)

    u1 = spread_rows(layer_norm(turn(my_fourth(x), flip).astype(F32))[0].astype(BF))
    oth = [None] * 7
    oth[4] = spread_weight(quarter(w_gate))
    for i in (1, 2, 0):
        oth[i] = swap_fsdp(own[i])
    oth[5] = spread_weight(quarter(w_up))
    oth[3] = swap_fsdp(w_attn_out)
    hf = w_down.shape[0] // 2
    oth[6] = jnp.concatenate(
        [swap_fsdp(w_down[:hf]), spread_weight(quarter(w_down[hf:]))], axis=0
    )
    xf = turn(x, flip).astype(F32)

    def into(u, i):
        return dot(u[:, :dh], own[i]) + dot(u[:, dh:], oth[i])

    def out_of(u, i):
        return jnp.concatenate([dot(u, own[i]), dot(u, oth[i])], axis=1)

    def out_back(g, i):
        return ndot(g[:, :dh], own[i]) + ndot(g[:, dh:], oth[i])

    values = into(u1, 2).astype(BF)
    qr, kr, context = attention_call(
        forward_body,
        lengths,
        (into(u1, 0), into(u1, 1), values),
        tables,
        3,
        0,
        "attention_forward",
    )
    def my_rows(v):
        picked = lax.dynamic_slice_in_dim(v.reshape(nseq, whole, -1), me * local, local, 1)
        return picked.reshape(rows, -1)

    keep = (places[None, :] < lengths[:, None]).astype(F32).reshape(rows, 1)
    dy = turn(cotangent.reshape(rows, width), flip).astype(F32) * keep
    dy_low = dy.astype(BF)
    h1 = xf + tp_total(lambda u: out_of(u, 3), my_rows(context))
    n2, rstd2 = layer_norm(h1)
    u2 = n2.astype(BF)
    gate = into(u2, 4)
    upper = into(u2, 5)
    sigma = jax.nn.sigmoid(gate)
    hidden = (gate * sigma * upper).astype(BF)

    def grads_into(u, g, parts):
        step = dh // parts
        return [
            (
                tdot(u[:, j * step : (j + 1) * step], g),
                tdot(u[:, dh + j * step : dh + (j + 1) * step], g).astype(BF),
            )
            for j in range(parts)
        ]

    def grads_out(u, g, parts):
        step = u.shape[1] // parts
        return [
            (
                tdot(u[:, j * step : (j + 1) * step], g[:, :dh]),
                tdot(u[:, j * step : (j + 1) * step], g[:, dh:]).astype(BF),
            )
            for j in range(parts)
        ]

    dhidden = out_back(dy_low, 6)
    dgate = (dhidden * upper * sigma * (1.0 + gate * (1.0 - sigma))).astype(BF)
    dupper = (dhidden * gate * sigma).astype(BF)

    def du2_of(dg, du):
        return jnp.concatenate(
            [ndot(dg, w[4]) + ndot(du, w[5]) for w in (own, oth)], axis=1
        )

    du2_half = tp_half(du2_of, dgate, dupper)
    mid = rows // 2
    odd = t & 1
    low = odd * mid + ((t >> 1) & 1) * fourth

    def fourth_at(v):
        return lax.dynamic_slice_in_dim(v, low, fourth, 0)

    da_part = fourth_at(dy) + norm_back(
        lax.dynamic_slice_in_dim(du2_half, ((t >> 1) & 1) * fourth, fourth, 0).astype(F32),
        fourth_at(n2),
        fourth_at(rstd2),
    )
    da = spread_rows(da_part.astype(BF))
    dh1 = dy + norm_back(tp_join(du2_half), n2, rstd2)
    hidden_late, da = lax.optimization_barrier((hidden, da))
    h2 = h1 + tp_total(lambda u: out_of(u, 6), hidden_late)
    out_block = turn((h2 * keep).astype(BF), flip)
    dcontext = out_back(da, 3).astype(BF)
    dq, dk, dv = attention_call(
        backward_body, lengths, (qr, kr, values, dcontext), tables, 3, 2, "attention_backward"
    )
    n1, rstd1 = layer_norm(xf)

    def gradient(pair):
        return pair[0] + swap_fsdp(pair[1]).astype(F32)

    g_attn = gradient(grads_out(context, da, 1)[0])
    g_value, g_key, g_query = [gradient(grads_into(u1, g, 1)[0]) for g in (dv, dk, dq)]

    def du1_of(q, k, v):
        return jnp.concatenate(
            [ndot(q, w[0]) + ndot(k, w[1]) + ndot(v, w[2]) for w in (own, oth)], axis=1
        )

    grad_input = turn(dh1 + norm_back(tp_total(du1_of, my_rows(dq), my_rows(dk), my_rows(dv)), n1, rstd1), flip)
    chunks = (
        grads_out(hidden, dy_low, 4)
        + grads_into(u2, dgate, 4)
        + grads_into(u2, dupper, 4)
    )
    totals = [None] * len(chunks)
    totals[0::2] = run_stream(chunks[0::2])
    totals[1::2] = run_stream(chunks[1::2])

    def lay(parts):
        rows_each = parts[0].shape[0]
        out = jnp.zeros((rows_each * len(parts), parts[0].shape[1]), F32)
        for j, p in enumerate(parts):
            out = lax.dynamic_update_slice_in_dim(out, p.astype(F32), j * rows_each, 0)
        return out

    g_down, g_gate, g_up = lay(totals[0:4]), lay(totals[4:8]), lay(totals[8:12])
    return (
        out_block.reshape(nseq, local, width),
        grad_input.reshape(nseq, local, width),
        g_query,
        g_key,
        g_value,
        g_attn,
        g_gate,
        g_up,
        g_down,
    )


def solution(mesh):
    return jax.shard_map(
        per_device,
        mesh=mesh,
        in_specs=(
            P("fsdp", "ctx", None),
            P("fsdp", "ctx", None),
            P("fsdp"),
            P("fsdp", "tp"),
            P("fsdp", "tp"),
            P("fsdp", "tp"),
            P("tp", "fsdp"),
            P("fsdp", "tp"),
            P("fsdp", "tp"),
            P("tp", "fsdp"),
        ),
        out_specs=(
            P("fsdp", "ctx", None),
            P("fsdp", "ctx", None),
            P("fsdp", "tp"),
            P("fsdp", "tp"),
            P("fsdp", "tp"),
            P("tp", "fsdp"),
            P("fsdp", "tp"),
            P("fsdp", "tp"),
            P("tp", "fsdp"),
        ),
        check_vma=False,
    )
```

```python
import jax
import jax.numpy as jnp
from jax import lax
from jax.experimental import pallas as pl
from jax.experimental.pallas import tpu as pltpu
from jax.sharding import PartitionSpec as P

HD = 128
BF = jnp.bfloat16
F32 = jnp.float32


def layer_norm(v):
    centered = v - jnp.mean(v, axis=-1, keepdims=True)
    rstd = lax.rsqrt(jnp.mean(centered * centered, axis=-1, keepdims=True) + 1e-05)
    return (centered * rstd, rstd)


def norm_back(grad, normed, rstd):
    return rstd * (
        grad
        - jnp.mean(grad, axis=-1, keepdims=True)
        - normed * jnp.mean(grad * normed, axis=-1, keepdims=True)
    )


def dot(left, right):
    return jnp.dot(left, right, preferred_element_type=F32)


def tdot(left, right):
    return lax.dot_general(left, right, (((0,), (0,)), ((), ())), preferred_element_type=F32)


def ndot(left, right):
    return lax.dot_general(left, right, (((1,), (1,)), ((), ())), preferred_element_type=F32)


def after(v, *others):
    return lax.optimization_barrier((v,) + others)[0]


def mm(left, right, dims):
    return lax.dot_general(left, right, (dims, ((), ())), preferred_element_type=F32)


def block_probs(q, k, length, first):
    span = (q.shape[0], k.shape[0])
    scores = mm(q, k, ((1,), (1,))) * (1.0 / HD**0.5)
    query = first + lax.broadcasted_iota(jnp.int32, span, 0)
    key = lax.broadcasted_iota(jnp.int32, span, 1)
    visible = (key <= query) & (key < length)
    masked = jnp.where(visible, scores, -1e30)
    top = jnp.max(masked, axis=-1, keepdims=True)
    expo = jnp.where(visible, jnp.exp(masked - top), 0.0)
    return expo / jnp.sum(expo, axis=-1, keepdims=True)


def forward_body(block, lens, qraw, kraw, v, cosine, sine, qr, kr, ctx):
    length = lens[pl.program_id(0)]
    for raw, out in ((qraw, qr), (kraw, kr)):
        x = raw[...]
        out[...] = (x * cosine[...] + pltpu.roll(x, HD // 2, 1) * sine[...]).astype(BF)
    for first in range(0, qr.shape[0], block):
        last = first + block
        probs = block_probs(qr[first:last, :], kr[:last, :], length, first).astype(BF)
        ctx[first:last, :] = mm(probs, v[:last, :], ((1,), (0,))).astype(BF)


def backward_body(block, lens, qr, kr, v, dctx, cosine, sine, dq, dk, dv, dk_sum, dv_sum):
    length = lens[pl.program_id(0)]
    factor = 1.0 / HD**0.5
    dk_sum[...] = jnp.zeros_like(dk_sum)
    dv_sum[...] = jnp.zeros_like(dv_sum)

    def unturn(x, c, s):
        return (x * c - pltpu.roll(x, HD // 2, 1) * s).astype(BF)

    for first in range(0, qr.shape[0], block):
        last = first + block
        q = qr[first:last, :]
        dc = dctx[first:last, :]
        k = kr[:last, :]
        probs = block_probs(q, k, length, first)
        dprobs = mm(dc, v[:last, :], ((1,), (1,)))
        delta = jnp.sum(probs * dprobs, axis=-1, keepdims=True)
        dscores = (probs * (dprobs - delta)).astype(BF)
        dq[first:last, :] = unturn(
            mm(dscores, k, ((1,), (0,))) * factor, cosine[first:last, :], sine[first:last, :]
        )
        dk_sum[:last, :] += mm(dscores, q, ((0,), (0,)))
        dv_sum[:last, :] += mm(probs.astype(BF), dc, ((0,), (0,)))
    dk[...] = unturn(dk_sum[...] * factor, cosine[...], sine[...])
    dv[...] = dv_sum[...].astype(BF)


def attention_call(body, lengths, arrays, tables, outs, scratch):
    rows, width = arrays[0].shape
    nseq = lengths.shape[0]
    whole = rows // nseq
    tile = pl.BlockSpec((whole, HD), lambda s, h, lens: (s, h))
    table = pl.BlockSpec((whole, HD), lambda s, h, lens: (0, 0))
    block = whole // 4
    return pl.pallas_call(
        lambda *refs: body(block, *refs),
        grid_spec=pltpu.PrefetchScalarGridSpec(
            num_scalar_prefetch=1,
            grid=(nseq, width // HD),
            in_specs=[tile] * len(arrays) + [table] * len(tables),
            out_specs=[tile] * outs,
            scratch_shapes=[pltpu.VMEM((whole, HD), F32)] * scratch,
        ),
        out_shape=[jax.ShapeDtypeStruct((rows, width), BF)] * outs,
    )(lengths, *arrays, *tables)


def swap_fsdp(v):
    return lax.ppermute(v, "fsdp", [(0, 1), (1, 0)])


def tp_swap(v, bit):
    n = lax.axis_size("tp")
    return lax.ppermute(v, "tp", [(i, i ^ bit) for i in range(n)])


def tp_half(make, *parts):
    n = lax.axis_size("tp")
    mid = parts[0].shape[0] // 2
    got = tp_swap(make(*(p[mid:] for p in parts)).astype(BF), 1)
    total = make(*(p[:mid] for p in parts)) + got.astype(F32)
    bit = 2
    while bit < n:
        sent = total.astype(BF)
        total = sent.astype(F32) + tp_swap(sent, bit).astype(F32)
        bit *= 2
    return total.astype(BF)


def tp_join(kept):
    return jnp.concatenate([kept, tp_swap(kept, 1)], axis=0).astype(F32)


class LineGather:
    def __init__(self, piece):
        self.piece = piece
        self.me = lax.axis_index("ctx")
        self.up1 = lax.ppermute(piece, "ctx", [(0, 1), (1, 2), (2, 3)])
        self.down1 = lax.ppermute(piece, "ctx", [(1, 0), (2, 1), (3, 2)])
        self.up2 = lax.ppermute(piece, "ctx", [(0, 2), (1, 3)])
        self.down2 = lax.ppermute(piece, "ctx", [(2, 0), (3, 1)])

    def finish(self, store, *held):
        me = self.me
        relay = jnp.where(me == 2, self.up2, self.down2)
        if held:
            relay = after(relay, *held)
        far = lax.ppermute(relay, "ctx", [(2, 3), (1, 0)])
        store(me, self.piece)
        store((me - 1) % 4, jnp.where(me >= 1, self.up1, far))
        store((me - 2) % 4, jnp.where(me >= 2, self.up2, self.down2))
        store((me - 3) % 4, jnp.where(me == 3, far, self.down1))


class Box:
    def __init__(self, shape, dtype):
        self.v = jnp.zeros(shape, dtype)

    def put(self, piece, *at):
        at = [jnp.asarray(a, jnp.int32) for a in at]
        at += [jnp.int32(0)] * (self.v.ndim - len(at))
        self.v = lax.dynamic_update_slice(self.v, piece.astype(self.v.dtype), at)


def quarter(w):
    part = w.shape[0] // lax.axis_size("ctx")
    return lax.dynamic_slice_in_dim(w, lax.axis_index("ctx") * part, part, 0)


class Rows:
    def __init__(self, piece):
        self.gather = LineGather(piece)
        self.line = Box((4,) + piece.shape, piece.dtype)

    def finish(self):
        half = (lax.axis_index("tp") >> 1) & 1
        self.gather.finish(lambda which, got: self.line.put(got[None], which))
        line = self.line.v
        other = tp_swap(line, 2)
        pair = Box((4, 2) + line.shape[1:], line.dtype)
        pair.put(line[:, None], 0, half)
        pair.put(other[:, None], 0, 1 - half)
        mine = pair.v.reshape(-1, line.shape[-1])
        return jnp.concatenate([mine, tp_swap(mine, 1)], axis=0)


class Stream:
    def __init__(self):
        self.chunks, self.done, self.tick = [], [], 0
        self.stage1, self.stage2, self.stage3 = {}, {}, {}

    def step(self, *extra):
        t, place = self.tick, lax.axis_index("ctx")
        send = {}
        if t < len(self.chunks):
            send["x"] = self.chunks[t][1]
        for name, held, lag in (("a", self.stage1, 1), ("b", self.stage2, 2), ("c", self.stage3, 3)):
            if t - lag in held:
                send[name] = held[t - lag]
        send, extra = lax.optimization_barrier((send, extra))
        if "c" in send:
            back = lax.ppermute(send["c"], "ctx", [(1, 0), (2, 3)])
            self.done.append(jnp.where((place == 0) | (place == 3), back, send["c"]))
        if "b" in send:
            got = lax.ppermute(send["b"], "ctx", [(1, 2), (2, 1)])
            self.stage3[t - 2] = (send["b"].astype(F32) + got.astype(F32)).astype(BF)
        if "a" in send:
            got = lax.ppermute(send["a"], "ctx", [(0, 1), (3, 2)])
            self.stage2[t - 1] = (send["a"].astype(F32) + got.astype(F32)).astype(BF)
        if "x" in send:
            got = swap_fsdp(send["x"])
            self.stage1[t] = (self.chunks[t][0] + got.astype(F32)).astype(BF)
        self.tick += 1
        return extra


def per_device(
    layer_input, cotangent, lengths, w_query, w_key, w_value, w_attn_out, w_gate, w_up, w_down
):
    nseq, local, width = layer_input.shape
    dh = width // 2
    rows = nseq * local
    whole = local * lax.axis_size("ctx")
    pair = lax.axis_index("fsdp")
    me = lax.axis_index("ctx")
    t = lax.axis_index("tp")
    core = t & 1
    fourth = rows // 4
    at_fourth = ((t >> 1) & 1) * fourth
    places = me * local + jnp.arange(local, dtype=jnp.int32)
    freqs = 10000.0 ** (-(jnp.arange(HD // 2, dtype=F32) * 2.0) / HD)
    angles = jnp.arange(whole, dtype=F32)[:, None] * freqs[None, :]
    cosine = jnp.cos(angles)
    sine = jnp.sin(angles)
    tables = (
        jnp.concatenate([cosine, cosine], axis=-1),
        jnp.concatenate([-sine, sine], axis=-1),
    )
    lens = jnp.stack(
        [lax.dynamic_index_in_dim(lengths, core, 0, False), lax.dynamic_index_in_dim(lengths, 1 - core, 0, False)]
    )

    def block_of(v, seq, start, size):
        return jnp.concatenate(
            [
                lax.dynamic_slice(v, (seq, start, side * dh), (1, size, dh))
                for side in (pair, 1 - pair)
            ],
            axis=-1,
        )[0]

    def arranged(v):
        return jnp.concatenate([block_of(v, s, 0, local) for s in (core, 1 - core)], axis=0)

    def restored(v, dtype):
        box = Box((nseq, local, width), dtype)
        for i, seq in enumerate((core, 1 - core)):
            for j, side in enumerate((pair, 1 - pair)):
                part = v[i * local : (i + 1) * local, j * dh : (j + 1) * dh]
                box.put(part[None], seq, 0, side * dh)
        return box.v

    u1_rows = Rows(
        layer_norm(block_of(layer_input, core, at_fourth, fourth).astype(F32))[0].astype(BF)
    )
    gate_part = swap_fsdp(quarter(w_gate))
    key_other = swap_fsdp(w_key)
    value_other = swap_fsdp(w_value)
    query_other = swap_fsdp(w_query)
    up_part = swap_fsdp(quarter(w_up))
    out_other = swap_fsdp(w_attn_out)
    hf = w_down.shape[0] // 2
    down_part = swap_fsdp(quarter(w_down[hf:]))
    down_other = swap_fsdp(w_down[:hf])

    gate_line = LineGather(gate_part)
    u1 = u1_rows.finish()
    full_q = jnp.concatenate([w_query, query_other], axis=0)
    full_k = jnp.concatenate([w_key, key_other], axis=0)
    full_v = jnp.concatenate([w_value, value_other], axis=0)
    full_o = jnp.concatenate([w_attn_out, out_other], axis=1)
    up_line = LineGather(after(up_part, u1))
    qraw = dot(u1, full_q)
    kraw = dot(u1, full_k)
    values = dot(u1, full_v).astype(BF)
    full_g, full_u = Box((width, w_gate.shape[1]), BF), Box((width, w_up.shape[1]), BF)
    part = dh // 4
    full_g.put(w_gate, 0)
    gate_line.finish(lambda which, got: full_g.put(got, dh + which * part), qraw, kraw, values)
    down_line = LineGather(after(down_part, qraw, kraw, values))
    qr, kr, context = attention_call(forward_body, lens, (qraw, kraw, values), tables, 3, 0)

    def my_rows(v):
        picked = lax.dynamic_slice_in_dim(v.reshape(nseq, whole, -1), me * local, local, 1)
        return picked.reshape(rows, -1)

    keep = jnp.concatenate([(places < lens[i]).astype(F32) for i in range(nseq)]).reshape(rows, 1)
    dy = arranged(cotangent).astype(F32) * keep
    dy_low = dy.astype(BF)
    xf = arranged(layer_input).astype(F32)
    attn_half = tp_half(lambda u: dot(u, full_o), my_rows(context))
    full_u.put(w_up, 0)
    up_line.finish(lambda which, got: full_u.put(got, dh + which * part), attn_half)
    full_d = Box((w_down.shape[0], width), BF)
    full_d.put(w_down, 0)
    full_d.put(down_other, 0, dh)
    down_line.finish(
        lambda which, got: full_d.put(got, hf + which * (hf // 4), dh), attn_half
    )
    h1 = xf + tp_join(attn_half)
    n2, rstd2 = layer_norm(h1)
    u2 = n2.astype(BF)
    gate = dot(u2, full_g.v)
    upper = dot(u2, full_u.v)
    sigma = jax.nn.sigmoid(gate)
    hidden = (gate * sigma * upper).astype(BF)

    def grads_into(u, g, parts):
        step = dh // parts
        return [
            (
                tdot(u[:, j * step : (j + 1) * step], g),
                tdot(u[:, dh + j * step : dh + (j + 1) * step], g).astype(BF),
            )
            for j in range(parts)
        ]

    def grads_out(u, g, parts):
        step = u.shape[1] // parts
        return [
            (
                tdot(u[:, j * step : (j + 1) * step], g[:, :dh]),
                tdot(u[:, j * step : (j + 1) * step], g[:, dh:]).astype(BF),
            )
            for j in range(parts)
        ]

    even, uneven = Stream(), Stream()

    def enqueue(chunks):
        even.chunks += chunks[0::2]
        uneven.chunks += chunks[1::2]

    enqueue(grads_out(hidden, dy_low, 4))
    (dy_next,) = even.step(dy_low)
    (dy_next,) = uneven.step(dy_next)
    dhidden = ndot(dy_next, full_d.v)
    dgate = (dhidden * upper * sigma * (1.0 + gate * (1.0 - sigma))).astype(BF)
    dupper = (dhidden * gate * sigma).astype(BF)
    enqueue(grads_into(u2, dgate, 4))
    enqueue(grads_into(u2, dupper, 4))
    du2_half = tp_half(
        lambda dg, du: ndot(dg, full_g.v) + ndot(du, full_u.v), dgate, dupper
    )
    even.step()
    uneven.step()

    def fourth_at(v):
        return lax.dynamic_slice_in_dim(v, at_fourth, fourth, 0)

    da_part = fourth_at(dy) + norm_back(
        fourth_at(du2_half).astype(F32), fourth_at(n2), fourth_at(rstd2)
    )
    (da_part,) = even.step(da_part.astype(BF))
    da_rows = Rows(da_part)
    uneven.step()
    even.step()
    uneven.step()
    da = da_rows.finish()
    (da,) = even.step(da)
    uneven.step()
    dcontext = ndot(da, full_o).astype(BF)
    dq, dk, dv = attention_call(backward_body, lens, (qr, kr, values, dcontext), tables, 3, 2)
    dq, dk, dv, hidden_late = even.step(dq, dk, dv, hidden)
    uneven.step()
    n1, rstd1 = layer_norm(xf)
    pairs = grads_out(context, da, 1) + [grads_into(u1, g, 1)[0] for g in (dv, dk, dq)]
    sent = even.step(*(p[1] for p in pairs))
    g_attn, g_value, g_key, g_query = [
        p[0] + swap_fsdp(s).astype(F32) for p, s in zip(pairs, sent)
    ]
    uneven.step()
    du1 = tp_join(
        tp_half(
            lambda q, k, v: ndot(q, full_q) + ndot(k, full_k) + ndot(v, full_v),
            my_rows(dq),
            my_rows(dk),
            my_rows(dv),
        )
    )
    h2 = h1 + tp_join(tp_half(lambda u: dot(u, full_d.v), hidden_late))
    even.step()
    uneven.step()
    even.step()
    uneven.step()
    dh1 = dy + norm_back(tp_join(du2_half), n2, rstd2)
    grad_input = restored(dh1 + norm_back(du1, n1, rstd1), F32)
    out_block = restored(h2 * keep, BF)
    totals = [None] * 12
    totals[0::2] = even.done
    totals[1::2] = uneven.done

    def lay(parts):
        box = Box((parts[0].shape[0] * len(parts), parts[0].shape[1]), F32)
        for j, p in enumerate(parts):
            box.put(p, j * p.shape[0])
        return box.v

    return (
        out_block,
        grad_input,
        g_query,
        g_key,
        g_value,
        g_attn,
        lay(totals[4:8]),
        lay(totals[8:12]),
        lay(totals[0:4]),
    )


def solution(mesh):
    return jax.shard_map(
        per_device,
        mesh=mesh,
        in_specs=(
            P("fsdp", "ctx", None),
            P("fsdp", "ctx", None),
            P("fsdp"),
            P("fsdp", "tp"),
            P("fsdp", "tp"),
            P("fsdp", "tp"),
            P("tp", "fsdp"),
            P("fsdp", "tp"),
            P("fsdp", "tp"),
            P("tp", "fsdp"),
        ),
        out_specs=(
            P("fsdp", "ctx", None),
            P("fsdp", "ctx", None),
            P("fsdp", "tp"),
            P("fsdp", "tp"),
            P("fsdp", "tp"),
            P("tp", "fsdp"),
            P("fsdp", "tp"),
            P("fsdp", "tp"),
            P("tp", "fsdp"),
        ),
        check_vma=False,
    )
```

```python
import jax
import jax.numpy as jnp
from jax import lax
from jax.experimental import pallas as pl
from jax.experimental.pallas import tpu as pltpu
from jax.sharding import PartitionSpec as P

HD = 128
BF = jnp.bfloat16
F32 = jnp.float32


def layer_norm(v):
    centered = v - jnp.mean(v, axis=-1, keepdims=True)
    rstd = lax.rsqrt(jnp.mean(centered * centered, axis=-1, keepdims=True) + 1e-05)
    return (centered * rstd, rstd)


def norm_back(grad, normed, rstd):
    return rstd * (
        grad
        - jnp.mean(grad, axis=-1, keepdims=True)
        - normed * jnp.mean(grad * normed, axis=-1, keepdims=True)
    )


def dot(left, right):
    return jnp.dot(left, right, preferred_element_type=F32)


def tdot(left, right):
    return lax.dot_general(left, right, (((0,), (0,)), ((), ())), preferred_element_type=F32)


def ndot(left, right):
    return lax.dot_general(left, right, (((1,), (1,)), ((), ())), preferred_element_type=F32)


def mm(left, right, dims):
    return lax.dot_general(left, right, (dims, ((), ())), preferred_element_type=F32)


def block_probs(q, k, length, first):
    span = (q.shape[0], k.shape[0])
    scores = mm(q, k, ((1,), (1,))) * (1.0 / HD**0.5)
    query = first + lax.broadcasted_iota(jnp.int32, span, 0)
    key = lax.broadcasted_iota(jnp.int32, span, 1)
    visible = (key <= query) & (key < length)
    masked = jnp.where(visible, scores, -1e30)
    top = jnp.max(masked, axis=-1, keepdims=True)
    expo = jnp.where(visible, jnp.exp(masked - top), 0.0)
    return expo / jnp.sum(expo, axis=-1, keepdims=True)


def forward_body(block, lens, qraw, kraw, vraw, cosine, sine, qr, kr, v, ctx):
    length = lens[pl.program_id(0)]
    v[...] = vraw[...].astype(BF)
    for raw, out in ((qraw, qr), (kraw, kr)):
        x = raw[...]
        out[...] = (x * cosine[...] + pltpu.roll(x, HD // 2, 1) * sine[...]).astype(BF)
    for first in range(0, qr.shape[0], block):
        last = first + block
        probs = block_probs(qr[first:last, :], kr[:last, :], length, first).astype(BF)
        ctx[first:last, :] = mm(probs, v[:last, :], ((1,), (0,))).astype(BF)


def backward_body(block, lens, qr, kr, v, dctx, cosine, sine, dq, dk, dv, dk_sum, dv_sum):
    length = lens[pl.program_id(0)]
    factor = 1.0 / HD**0.5
    dk_sum[...] = jnp.zeros_like(dk_sum)
    dv_sum[...] = jnp.zeros_like(dv_sum)

    def unturn(x, c, s):
        return (x * c - pltpu.roll(x, HD // 2, 1) * s).astype(BF)

    for first in range(0, qr.shape[0], block):
        last = first + block
        q = qr[first:last, :]
        dc = dctx[first:last, :]
        k = kr[:last, :]
        probs = block_probs(q, k, length, first)
        dprobs = mm(dc, v[:last, :], ((1,), (1,)))
        delta = jnp.sum(probs * dprobs, axis=-1, keepdims=True)
        dscores = (probs * (dprobs - delta)).astype(BF)
        dq[first:last, :] = unturn(
            mm(dscores, k, ((1,), (0,))) * factor, cosine[first:last, :], sine[first:last, :]
        )
        dk_sum[:last, :] += mm(dscores, q, ((0,), (0,)))
        dv_sum[:last, :] += mm(probs.astype(BF), dc, ((0,), (0,)))
    dk[...] = unturn(dk_sum[...] * factor, cosine[...], sine[...])
    dv[...] = dv_sum[...].astype(BF)


def attention_call(body, lengths, arrays, tables, outs, scratch, thirds=False):
    rows, width = arrays[0].shape
    if thirds:
        width //= 3
    nseq = lengths.shape[0]
    whole = rows // nseq
    heads = width // HD
    tile = pl.BlockSpec((whole, HD), lambda s, h, lens: (s, h))
    tiles = [tile] * len(arrays)
    if thirds:
        tiles = [
            pl.BlockSpec((whole, HD), lambda s, h, lens, i=i: (s, h + i * heads)) for i in range(3)
        ]
    table = pl.BlockSpec((whole, HD), lambda s, h, lens: (0, 0))
    block = whole // 4
    return pl.pallas_call(
        lambda *refs: body(block, *refs),
        grid_spec=pltpu.PrefetchScalarGridSpec(
            num_scalar_prefetch=1,
            grid=(nseq, heads),
            in_specs=tiles + [table] * len(tables),
            out_specs=[tile] * outs,
            scratch_shapes=[pltpu.VMEM((whole, HD), F32)] * scratch,
        ),
        out_shape=[jax.ShapeDtypeStruct((rows, width), BF)] * outs,
    )(lengths, *arrays, *tables)


def swap_fsdp(v):
    return lax.ppermute(v, "fsdp", [(0, 1), (1, 0)])


def tp_swap(v, bit):
    n = lax.axis_size("tp")
    return lax.ppermute(v, "tp", [(i, i ^ bit) for i in range(n)])


def tp_half(term):
    n = lax.axis_size("tp")
    mid = term.shape[0] // 2
    got = tp_swap(term[mid:].astype(BF), 1)
    total = term[:mid] + got.astype(F32)
    bit = 2
    while bit < n:
        sent = total.astype(BF)
        total = sent.astype(F32) + tp_swap(sent, bit).astype(F32)
        bit *= 2
    return total.astype(BF)


def tp_join(kept):
    return jnp.concatenate([kept, tp_swap(kept, 1)], axis=0).astype(F32)


class LineGather:
    def __init__(self, piece):
        self.piece = piece
        self.up1 = lax.ppermute(piece, "ctx", [(0, 1), (1, 2), (2, 3)])
        self.down1 = lax.ppermute(piece, "ctx", [(1, 0), (2, 1), (3, 2)])
        self.up2 = lax.ppermute(piece, "ctx", [(0, 2), (1, 3)])
        self.down2 = lax.ppermute(piece, "ctx", [(2, 0), (3, 1)])

    def finish(self, store):
        me = lax.axis_index("ctx")
        relay = jnp.where(me == 2, self.up2, self.down2)
        far = lax.ppermute(relay, "ctx", [(2, 3), (1, 0)])
        store(me, self.piece)
        store((me - 1) % 4, jnp.where(me >= 1, self.up1, far))
        store((me - 2) % 4, jnp.where(me >= 2, self.up2, self.down2))
        store((me - 3) % 4, jnp.where(me == 3, far, self.down1))


class Box:
    def __init__(self, shape, dtype):
        self.v = jnp.zeros(shape, dtype)

    def put(self, piece, *at):
        at = [jnp.asarray(a, jnp.int32) for a in at]
        at += [jnp.int32(0)] * (self.v.ndim - len(at))
        self.v = lax.dynamic_update_slice(self.v, piece.astype(self.v.dtype), at)


def quarter(w):
    part = w.shape[0] // lax.axis_size("ctx")
    return lax.dynamic_slice_in_dim(w, lax.axis_index("ctx") * part, part, 0)


class Rows:
    def __init__(self, piece):
        self.gather = LineGather(piece)
        self.line = Box((4,) + piece.shape, piece.dtype)

    def finish(self):
        half = (lax.axis_index("tp") >> 1) & 1
        self.gather.finish(lambda which, got: self.line.put(got[None], which))
        line = self.line.v
        other = tp_swap(line, 2)
        pair = Box((4, 2) + line.shape[1:], line.dtype)
        pair.put(line[:, None], 0, half)
        pair.put(other[:, None], 0, 1 - half)
        mine = pair.v.reshape(-1, line.shape[-1])
        return mine, tp_swap(mine, 1)


def reduce_chunks(chunks):
    place = lax.axis_index("ctx")
    edge = (place == 0) | (place == 3)
    done = []
    for own, other in chunks:
        got = swap_fsdp(other)
        v = (own() + got.astype(F32)).astype(BF)
        got = lax.ppermute(v, "ctx", [(0, 1), (3, 2)])
        v = (v.astype(F32) + got.astype(F32)).astype(BF)
        got = lax.ppermute(v, "ctx", [(1, 2), (2, 1)])
        v = (v.astype(F32) + got.astype(F32)).astype(BF)
        got = lax.ppermute(v, "ctx", [(1, 0), (2, 3)])
        done.append(jnp.where(edge, got, v))
    return done


def layer(
    layer_input, cotangent, lengths, w_query, w_key, w_value, w_attn_out, w_gate, w_up, w_down
):
    nseq, local, width = layer_input.shape
    dh = width // 2
    ff = w_gate.shape[1]
    rows = nseq * local
    whole = local * lax.axis_size("ctx")
    pair = lax.axis_index("fsdp")
    me = lax.axis_index("ctx")
    t = lax.axis_index("tp")
    core = t & 1
    fourth = rows // 4
    at_fourth = ((t >> 1) & 1) * fourth
    places = me * local + jnp.arange(local, dtype=jnp.int32)
    freqs = 10000.0 ** (-(jnp.arange(HD // 2, dtype=F32) * 2.0) / HD)
    angles = jnp.arange(whole, dtype=F32)[:, None] * freqs[None, :]
    cosine = jnp.cos(angles)
    sine = jnp.sin(angles)
    tables = (
        jnp.concatenate([cosine, cosine], axis=-1),
        jnp.concatenate([-sine, sine], axis=-1),
    )
    lens = jnp.stack(
        [lax.dynamic_index_in_dim(lengths, core, 0, False), lax.dynamic_index_in_dim(lengths, 1 - core, 0, False)]
    )

    def block_of(v, seq, start, size):
        return jnp.concatenate(
            [
                lax.dynamic_slice(v, (seq, start, side * dh), (1, size, dh))
                for side in (pair, 1 - pair)
            ],
            axis=-1,
        )[0]

    def arranged(v):
        return jnp.concatenate([block_of(v, s, 0, local) for s in (core, 1 - core)], axis=0)

    def restored(v, dtype):
        box = Box((nseq, local, width), dtype)
        for i, seq in enumerate((core, 1 - core)):
            for j, side in enumerate((pair, 1 - pair)):
                part = v[i * local : (i + 1) * local, j * dh : (j + 1) * dh]
                box.put(part[None], seq, 0, side * dh)
        return box.v

    gate_part = swap_fsdp(quarter(w_gate))
    key_other = swap_fsdp(w_key)
    value_other = swap_fsdp(w_value)
    query_other = swap_fsdp(w_query)
    up_part = swap_fsdp(quarter(w_up))
    out_other = swap_fsdp(w_attn_out)
    down_other = swap_fsdp(w_down)
    u1 = jnp.concatenate(Rows(
        layer_norm(block_of(layer_input, core, at_fourth, fourth).astype(F32))[0].astype(BF)
    ).finish(), axis=0)
    gate_line = LineGather(gate_part)
    up_line = LineGather(up_part)
    full_qkv = jnp.concatenate(
        [
            jnp.concatenate([w_query, query_other], axis=0),
            jnp.concatenate([w_key, key_other], axis=0),
            jnp.concatenate([w_value, value_other], axis=0),
        ],
        axis=1,
    )
    full_o = jnp.concatenate([w_attn_out, out_other], axis=1)
    raw = dot(u1, full_qkv)
    full_gu = Box((width, 2 * ff), BF)
    full_d = Box((ff, width), BF)
    part = dh // 4
    full_gu.put(w_gate, 0)
    full_gu.put(w_up, 0, ff)
    full_d.put(w_down, 0)
    gate_line.finish(lambda which, got: full_gu.put(got, dh + which * part))
    qr, kr, values, context = attention_call(
        forward_body, lens, (raw, raw, raw), tables, 4, 0, thirds=True
    )

    def my_rows(v):
        picked = lax.dynamic_slice_in_dim(v.reshape(nseq, whole, -1), me * local, local, 1)
        return picked.reshape(rows, -1)

    keep = jnp.concatenate([(places < lens[i]).astype(F32) for i in range(nseq)]).reshape(rows, 1)
    dy = arranged(cotangent).astype(F32) * keep
    dy_low = dy.astype(BF)
    xf = arranged(layer_input).astype(F32)
    h1 = xf + tp_join(tp_half(dot(my_rows(context), full_o)))
    up_line.finish(lambda which, got: full_gu.put(got, dh + which * part, ff))
    full_d.put(down_other, 0, dh)
    n2, rstd2 = layer_norm(h1)
    u2 = n2.astype(BF)
    both = dot(u2, full_gu.v)
    gate, upper = both[:, :ff], both[:, ff:]
    hidden = (gate * jax.nn.sigmoid(gate) * upper).astype(BF)

    def grads_into(u, g, parts):
        step = dh // parts
        return [
            (
                lambda j=j: tdot(u[:, j * step : (j + 1) * step], g),
                tdot(u[:, dh + j * step : dh + (j + 1) * step], g).astype(BF),
            )
            for j in range(parts)
        ]

    def grads_out(u, g, parts):
        step = u.shape[1] // parts
        return [
            (
                lambda j=j: tdot(u[:, j * step : (j + 1) * step], g[:, :dh]),
                tdot(u[:, j * step : (j + 1) * step], g[:, dh:]).astype(BF),
            )
            for j in range(parts)
        ]

    hidden, gate, upper = lax.optimization_barrier((hidden, gate, upper))
    sigma = jax.nn.sigmoid(gate)
    dhidden = ndot(dy_low, full_d.v)
    dgate = (dhidden * upper * sigma * (1.0 + gate * (1.0 - sigma))).astype(BF)
    dupper = (dhidden * gate * sigma).astype(BF)
    du2_half = tp_half(ndot(jnp.concatenate([dgate, dupper], axis=1), full_gu.v))
    chunks = grads_out(hidden, dy_low, 4) + grads_into(u2, dgate, 4) + grads_into(u2, dupper, 4)
    totals = [None] * 12
    totals[0::2] = reduce_chunks(chunks[0::2])
    totals[1::2] = reduce_chunks(chunks[1::2])

    def fourth_at(v):
        return lax.dynamic_slice_in_dim(v, at_fourth, fourth, 0)

    da_part = fourth_at(dy) + norm_back(
        fourth_at(du2_half).astype(F32), fourth_at(n2), fourth_at(rstd2)
    )
    das = Rows(da_part.astype(BF)).finish()
    grads = []
    for i, part in enumerate(das):
        cut = slice(i * whole, (i + 1) * whole)
        dcontext = ndot(part, full_o).astype(BF)
        grads.append(
            attention_call(
                backward_body,
                lens[i : i + 1],
                (qr[cut], kr[cut], values[cut], dcontext),
                tables,
                3,
                2,
            )
        )
    da = jnp.concatenate(das, axis=0)
    dq, dk, dv = [jnp.concatenate(parts, axis=0) for parts in zip(*grads)]
    n1, rstd1 = layer_norm(xf)
    made = [(grads_out, context, da)] + [(grads_into, u1, g) for g in (dv, dk, dq)]
    summed = []
    for maker, left, right in made:
        ((own, other),) = maker(left, right, 1)
        got = swap_fsdp(other)
        summed.append(own() + got.astype(F32))
    g_attn, g_value, g_key, g_query = summed
    term = ndot(
        jnp.concatenate([my_rows(dq), my_rows(dk), my_rows(dv)], axis=1), full_qkv
    )
    du1 = tp_join(tp_half(term))
    h2 = h1 + tp_join(tp_half(dot(hidden, full_d.v)))
    dh1 = dy + norm_back(tp_join(du2_half), n2, rstd2)
    grad_input = restored(dh1 + norm_back(du1, n1, rstd1), F32)
    out_block = restored(h2 * keep, BF)

    def lay(parts):
        box = Box((parts[0].shape[0] * len(parts), parts[0].shape[1]), F32)
        for j, p in enumerate(parts):
            box.put(p, j * p.shape[0])
        return box.v

    return (
        out_block,
        grad_input,
        g_query,
        g_key,
        g_value,
        g_attn,
        lay(totals[4:8]),
        lay(totals[8:12]),
        lay(totals[0:4]),
    )


def solution(mesh):
    return jax.shard_map(
        layer,
        mesh=mesh,
        in_specs=(
            P("fsdp", "ctx", None),
            P("fsdp", "ctx", None),
            P("fsdp"),
            P("fsdp", "tp"),
            P("fsdp", "tp"),
            P("fsdp", "tp"),
            P("tp", "fsdp"),
            P("fsdp", "tp"),
            P("fsdp", "tp"),
            P("tp", "fsdp"),
        ),
        out_specs=(
            P("fsdp", "ctx", None),
            P("fsdp", "ctx", None),
            P("fsdp", "tp"),
            P("fsdp", "tp"),
            P("fsdp", "tp"),
            P("tp", "fsdp"),
            P("fsdp", "tp"),
            P("fsdp", "tp"),
            P("tp", "fsdp"),
        ),
        check_vma=False,
    )
```

```python
import jax
import jax.numpy as jnp
from jax import lax
from jax.experimental import pallas as pl
from jax.experimental.pallas import tpu as pltpu
from jax.sharding import PartitionSpec as P

HD = 128
BF = jnp.bfloat16
F32 = jnp.float32


def layer_norm(v):
    centered = v - jnp.mean(v, axis=-1, keepdims=True)
    rstd = lax.rsqrt(jnp.mean(centered * centered, axis=-1, keepdims=True) + 1e-05)
    return (centered * rstd, rstd)


def norm_back(grad, normed, rstd):
    return rstd * (
        grad
        - jnp.mean(grad, axis=-1, keepdims=True)
        - normed * jnp.mean(grad * normed, axis=-1, keepdims=True)
    )


def dot(left, right):
    return jnp.dot(left, right, preferred_element_type=F32)


def tdot(left, right):
    return lax.dot_general(left, right, (((0,), (0,)), ((), ())), preferred_element_type=F32)


def ndot(left, right):
    return lax.dot_general(left, right, (((1,), (1,)), ((), ())), preferred_element_type=F32)


def mm(left, right, dims):
    return lax.dot_general(left, right, (dims, ((), ())), preferred_element_type=F32)


def block_probs(q, k, length, first):
    span = (q.shape[0], k.shape[0])
    scores = mm(q, k, ((1,), (1,))) * (1.0 / HD**0.5)
    query = first + lax.broadcasted_iota(jnp.int32, span, 0)
    key = lax.broadcasted_iota(jnp.int32, span, 1)
    visible = (key <= query) & (key < length)
    masked = jnp.where(visible, scores, -1e30)
    top = jnp.max(masked, axis=-1, keepdims=True)
    expo = jnp.where(visible, jnp.exp(masked - top), 0.0)
    return expo / jnp.sum(expo, axis=-1, keepdims=True)


def forward_body(block, start, lens, qraw, kraw, vraw, cosine, sine, qr, kr, v, ctx):
    length = lens[start + pl.program_id(0)]
    v[...] = vraw[...].astype(BF)
    for raw, out in ((qraw, qr), (kraw, kr)):
        x = raw[...]
        out[...] = (x * cosine[...] + pltpu.roll(x, HD // 2, 1) * sine[...]).astype(BF)
    for first in range(0, qr.shape[0], block):
        last = first + block
        probs = block_probs(qr[first:last, :], kr[:last, :], length, first).astype(BF)
        ctx[first:last, :] = mm(probs, v[:last, :], ((1,), (0,))).astype(BF)


def backward_body(block, start, lens, qr, kr, v, dctx, cosine, sine, dq, dk, dv, dk_sum, dv_sum):
    length = lens[start + pl.program_id(0)]
    factor = 1.0 / HD**0.5
    dk_sum[...] = jnp.zeros_like(dk_sum)
    dv_sum[...] = jnp.zeros_like(dv_sum)

    def unturn(x, c, s):
        return (x * c - pltpu.roll(x, HD // 2, 1) * s).astype(BF)

    for first in range(0, qr.shape[0], block):
        last = first + block
        q = qr[first:last, :]
        dc = dctx[first:last, :]
        k = kr[:last, :]
        probs = block_probs(q, k, length, first)
        dprobs = mm(dc, v[:last, :], ((1,), (1,)))
        delta = jnp.sum(probs * dprobs, axis=-1, keepdims=True)
        dscores = (probs * (dprobs - delta)).astype(BF)
        dq[first:last, :] = unturn(
            mm(dscores, k, ((1,), (0,))) * factor, cosine[first:last, :], sine[first:last, :]
        )
        dk_sum[:last, :] += mm(dscores, q, ((0,), (0,)))
        dv_sum[:last, :] += mm(probs.astype(BF), dc, ((0,), (0,)))
    dk[...] = unturn(dk_sum[...] * factor, cosine[...], sine[...])
    dv[...] = dv_sum[...].astype(BF)


def attention_call(body, lengths, arrays, tables, outs, scratch, seqs, thirds=False):
    rows, width = arrays[0].shape
    if thirds:
        width //= 3
    whole = rows // lengths.shape[0]
    heads = width // HD
    start, count = seqs

    def tile(offset, column):
        return pl.BlockSpec((whole, HD), lambda s, h, lens: (s + offset, h + column))

    if thirds:
        tiles = [tile(start, i * heads) for i in range(3)]
    else:
        tiles = [tile(start if v.shape[0] == rows else 0, 0) for v in arrays]
    table = pl.BlockSpec((whole, HD), lambda s, h, lens: (0, 0))
    block = whole // 4
    return pl.pallas_call(
        lambda *refs: body(block, start, *refs),
        grid_spec=pltpu.PrefetchScalarGridSpec(
            num_scalar_prefetch=1,
            grid=(count, heads),
            in_specs=tiles + [table] * len(tables),
            out_specs=[tile(0, 0)] * outs,
            scratch_shapes=[pltpu.VMEM((whole, HD), F32)] * scratch,
        ),
        out_shape=[jax.ShapeDtypeStruct((count * whole, width), BF)] * outs,
    )(lengths, *arrays, *tables)


def swap_fsdp(v):
    return lax.ppermute(v, "fsdp", [(0, 1), (1, 0)])


def tp_swap(v, bit):
    n = lax.axis_size("tp")
    return lax.ppermute(v, "tp", [(i, i ^ bit) for i in range(n)])


def tp_half(term):
    n = lax.axis_size("tp")
    mid = term.shape[0] // 2
    got = tp_swap(term[mid:].astype(BF), 1)
    sent = (term[:mid] + got.astype(F32)).astype(BF)
    bit = 2
    while bit < n:
        got = tp_swap(sent, bit)
        sent = (sent.astype(F32) + got.astype(F32)).astype(BF)
        bit *= 2
    return sent


def tp_join(kept):
    return jnp.concatenate([kept, tp_swap(kept, 1)], axis=0).astype(F32)


class LineGather:
    def __init__(self, piece):
        n = lax.axis_size("ctx")
        self.got = [piece]
        for far in range(1, n):
            pairs = [(i, (i + far) % n) for i in range(n)]
            self.got.append(lax.ppermute(piece, "ctx", pairs))

    def finish(self, store):
        me = lax.axis_index("ctx")
        for far, got in enumerate(self.got):
            store((me - far) % len(self.got), got)


class Box:
    def __init__(self, shape, dtype):
        self.v = jnp.zeros(shape, dtype)

    def put(self, piece, *at):
        at = [jnp.asarray(a, jnp.int32) for a in at]
        at += [jnp.int32(0)] * (self.v.ndim - len(at))
        self.v = lax.dynamic_update_slice(self.v, piece.astype(self.v.dtype), at)


def quarter(w):
    part = w.shape[0] // lax.axis_size("ctx")
    return lax.dynamic_slice_in_dim(w, lax.axis_index("ctx") * part, part, 0)


class Rows:
    def __init__(self, piece):
        self.gather = LineGather(piece)
        self.line = Box((4,) + piece.shape, piece.dtype)

    def finish(self):
        half = (lax.axis_index("tp") >> 1) & 1
        self.gather.finish(lambda which, got: self.line.put(got[None], which))
        line = self.line.v
        other = tp_swap(line, 2)
        pair = Box((4, 2) + line.shape[1:], line.dtype)
        pair.put(line[:, None], 0, half)
        pair.put(other[:, None], 0, 1 - half)
        mine = pair.v.reshape(-1, line.shape[-1])
        return mine, tp_swap(mine, 1)


def reduce_chunks(chunks):
    place = lax.axis_index("ctx")
    edge = (place == 0) | (place == 3)
    n = len(chunks)
    first, inner, crossed, done = {}, {}, {}, []
    for tick in range(n + 3):
        a, b, c = tick - 1, tick - 2, tick - 3
        total = sent = None
        pairs = [(0, 1), (1, 0), (2, 3), (3, 2)]
        if c in crossed:
            sent = total = (inner[c].astype(F32) + crossed[c].astype(F32)).astype(BF)
        if a in first:
            alone = total is None or total.shape != first[a].shape
            sent = first[a] if alone else jnp.where(edge, first[a], total)
        if sent is not None:
            got = lax.ppermute(sent, "ctx", pairs)
        if total is not None:
            back = got if total.shape == sent.shape else lax.ppermute(total, "ctx", pairs)
            done.append(jnp.where(edge, back, total))
        if b in inner:
            crossed[b] = lax.ppermute(inner[b], "ctx", [(1, 2), (2, 1)])
        if a in first:
            inner[a] = (first[a].astype(F32) + got.astype(F32)).astype(BF)
        if tick < n:
            own, other = chunks[tick]
            got = swap_fsdp(other)
            first[tick] = (own() + got.astype(F32)).astype(BF)
    return done


def layer(
    layer_input, cotangent, lengths, w_query, w_key, w_value, w_attn_out, w_gate, w_up, w_down
):
    nseq, local, width = layer_input.shape
    dh = width // 2
    ff = w_gate.shape[1]
    rows = nseq * local
    whole = local * lax.axis_size("ctx")
    pair = lax.axis_index("fsdp")
    me = lax.axis_index("ctx")
    t = lax.axis_index("tp")
    core = t & 1
    fourth = rows // 4
    at_fourth = ((t >> 1) & 1) * fourth
    places = me * local + jnp.arange(local, dtype=jnp.int32)
    freqs = 10000.0 ** (-(jnp.arange(HD // 2, dtype=F32) * 2.0) / HD)
    angles = jnp.arange(whole, dtype=F32)[:, None] * freqs[None, :]
    cosine = jnp.cos(angles)
    sine = jnp.sin(angles)
    tables = (
        jnp.concatenate([cosine, cosine], axis=-1),
        jnp.concatenate([-sine, sine], axis=-1),
    )
    lens = jnp.stack(
        [lax.dynamic_index_in_dim(lengths, core, 0, False), lax.dynamic_index_in_dim(lengths, 1 - core, 0, False)]
    )

    def block_of(v, seq, start, size):
        return jnp.concatenate(
            [
                lax.dynamic_slice(v, (seq, start, side * dh), (1, size, dh))
                for side in (pair, 1 - pair)
            ],
            axis=-1,
        )[0]

    def arranged(v):
        return jnp.concatenate([block_of(v, s, 0, local) for s in (core, 1 - core)], axis=0)

    def restored(v, dtype):
        box = Box((nseq, local, width), dtype)
        for i, seq in enumerate((core, 1 - core)):
            for j, side in enumerate((pair, 1 - pair)):
                part = v[i * local : (i + 1) * local, j * dh : (j + 1) * dh]
                box.put(part[None], seq, 0, side * dh)
        return box.v

    gate_part = swap_fsdp(quarter(w_gate))
    up_part = swap_fsdp(quarter(w_up))
    key_other = swap_fsdp(w_key)
    value_other = swap_fsdp(w_value)
    query_other = swap_fsdp(w_query)
    out_other = swap_fsdp(w_attn_out)
    down_other = swap_fsdp(w_down)
    u1 = jnp.concatenate(Rows(
        layer_norm(block_of(layer_input, core, at_fourth, fourth).astype(F32))[0].astype(BF)
    ).finish(), axis=0)
    gate_line = LineGather(gate_part)
    up_line = LineGather(up_part)
    full_qkv = jnp.concatenate(
        [
            jnp.concatenate([w_query, query_other], axis=0),
            jnp.concatenate([w_key, key_other], axis=0),
            jnp.concatenate([w_value, value_other], axis=0),
        ],
        axis=1,
    )
    full_o = jnp.concatenate([w_attn_out, out_other], axis=1)
    raw = dot(u1, full_qkv)
    full_gu = Box((width, 2 * ff), BF)
    full_d = Box((ff, width), BF)
    part = dh // 4
    full_gu.put(w_gate, 0)
    full_gu.put(w_up, 0, ff)
    full_d.put(w_down, 0)
    gate_line.finish(lambda which, got: full_gu.put(got, dh + which * part))
    qr, kr, values, context = attention_call(
        forward_body, lens, (raw, raw, raw), tables, 4, 0, (0, nseq), thirds=True
    )

    def my_rows(v):
        picked = lax.dynamic_slice_in_dim(v.reshape(nseq, whole, -1), me * local, local, 1)
        return picked.reshape(rows, -1)

    keep = jnp.concatenate([(places < lens[i]).astype(F32) for i in range(nseq)]).reshape(rows, 1)
    dy = arranged(cotangent).astype(F32) * keep
    dy_low = dy.astype(BF)
    xf = arranged(layer_input).astype(F32)
    h1 = xf + tp_join(tp_half(dot(my_rows(context), full_o)))
    up_line.finish(lambda which, got: full_gu.put(got, dh + which * part, ff))
    full_d.put(down_other, 0, dh)
    n2, rstd2 = layer_norm(h1)
    u2 = n2.astype(BF)
    both = dot(u2, full_gu.v)
    gate, upper = both[:, :ff], both[:, ff:]
    hidden = (gate * jax.nn.sigmoid(gate) * upper).astype(BF)

    def grads_into(u, g, high, wide):
        step, span = dh // high, g.shape[1] // wide
        return [
            (
                lambda j=j, k=k: tdot(
                    u[:, j * step : (j + 1) * step], g[:, k * span : (k + 1) * span]
                ),
                tdot(
                    u[:, dh + j * step : dh + (j + 1) * step], g[:, k * span : (k + 1) * span]
                ).astype(BF),
            )
            for j in range(high)
            for k in range(wide)
        ]

    def grads_out(u, g, parts, wide=1):
        step = u.shape[1] // parts
        return [
            (
                lambda j=j: tdot(u[:, j * step : (j + 1) * step], g[:, :dh]),
                tdot(u[:, j * step : (j + 1) * step], g[:, dh:]).astype(BF),
            )
            for j in range(parts)
        ]

    hidden, both = lax.optimization_barrier((hidden, both))
    gate, upper = both[:, :ff], both[:, ff:]
    sigma = jax.nn.sigmoid(gate)
    dhidden = ndot(dy_low, full_d.v)
    dgate = (dhidden * upper * sigma * (1.0 + gate * (1.0 - sigma))).astype(BF)
    dupper = (dhidden * gate * sigma).astype(BF)
    du2_half = tp_half(ndot(jnp.concatenate([dgate, dupper], axis=1), full_gu.v))
    chunks = grads_out(hidden, dy_low, 4) + grads_into(u2, dgate, 2, 2) + grads_into(u2, dupper, 2, 2)
    totals = [None] * 12
    totals[0::2] = reduce_chunks(chunks[0::2])
    totals[1::2] = reduce_chunks(chunks[1::2])

    def fourth_at(v):
        return lax.dynamic_slice_in_dim(v, at_fourth, fourth, 0)

    da_part = fourth_at(dy) + norm_back(
        fourth_at(du2_half).astype(F32), fourth_at(n2), fourth_at(rstd2)
    )
    das = Rows(da_part.astype(BF)).finish()
    grads = []
    for i, part in enumerate(das):
        dcontext = ndot(part, full_o).astype(BF)
        grads.append(
            attention_call(backward_body, lens, (qr, kr, values, dcontext), tables, 3, 2, (i, 1))
        )
    da = jnp.concatenate(das, axis=0)
    dq, dk, dv = [jnp.concatenate(parts, axis=0) for parts in zip(*grads)]
    n1, rstd1 = layer_norm(xf)
    made = [(grads_out, context, da)] + [(grads_into, u1, g) for g in (dv, dk, dq)]
    summed = []
    for maker, left, right in made:
        ((own, other),) = maker(left, right, 1, 1)
        got = swap_fsdp(other)
        summed.append(own() + got.astype(F32))
    g_attn, g_value, g_key, g_query = summed
    term = ndot(
        jnp.concatenate([my_rows(dq), my_rows(dk), my_rows(dv)], axis=1), full_qkv
    )
    du1 = tp_join(tp_half(term))
    h2 = h1 + tp_join(tp_half(dot(hidden, full_d.v)))
    out_block = restored(h2 * keep, BF)
    dh1 = dy + norm_back(tp_join(du2_half), n2, rstd2)
    grad_input = restored(dh1 + norm_back(du1, n1, rstd1), F32)

    def lay(parts, wide):
        rows_each, span = parts[0].shape
        box = Box((rows_each * len(parts) // wide, span * wide), F32)
        for j, p in enumerate(parts):
            box.put(p, j // wide * rows_each, j % wide * span)
        return box.v

    return (
        out_block,
        grad_input,
        g_query,
        g_key,
        g_value,
        g_attn,
        lay(totals[4:8], 2),
        lay(totals[8:12], 2),
        lay(totals[0:4], 1),
    )


def solution(mesh):
    return jax.shard_map(
        layer,
        mesh=mesh,
        in_specs=(
            P("fsdp", "ctx", None),
            P("fsdp", "ctx", None),
            P("fsdp"),
            P("fsdp", "tp"),
            P("fsdp", "tp"),
            P("fsdp", "tp"),
            P("tp", "fsdp"),
            P("fsdp", "tp"),
            P("fsdp", "tp"),
            P("tp", "fsdp"),
        ),
        out_specs=(
            P("fsdp", "ctx", None),
            P("fsdp", "ctx", None),
            P("fsdp", "tp"),
            P("fsdp", "tp"),
            P("fsdp", "tp"),
            P("tp", "fsdp"),
            P("fsdp", "tp"),
            P("fsdp", "tp"),
            P("tp", "fsdp"),
        ),
        check_vma=False,
    )
```
